32 devices in a mesh: sx: 4 (over z), sy: 4 (over y, x), dp: 2 (over core).
Axes of the slice: x: 2, y: 2, z: 4, core: 2. Of those that a mesh axis runs over, the one named last changes fastest.
Arguments:
- features: bfloat16 [2, 32, 32, 4, 8, 128], P('dp', 'sx', 'sy'), may hold values from -6 to 6
- cotangent: bfloat16 [2, 32, 32, 4, 8, 128], P('dp', 'sx', 'sy'), may hold values from -6 to 6
- first_weight: bfloat16 [27, 128, 128], replicated, may hold values from -0.109375 to 0.109375
- second_weight: bfloat16 [27, 128, 128], replicated, may hold values from -0.109375 to 0.109375
- neighbours: int32 [2, 4, 4, 4, 26], P('dp', 'sx', 'sy'), may hold values from -1 to 3, as said below
- counts: int32 [2, 4, 4], P('dp', 'sx', 'sy'), may hold values from 1 to 4, as said below
Outputs:
- out_field: bfloat16 [2, 32, 32, 4, 8, 128], P('dp', 'sx', 'sy')
- grad_input: bfloat16 [2, 32, 32, 4, 8, 128], P('dp', 'sx', 'sy')
- grad_first: float32 [27, 128, 128], replicated
- grad_second: float32 [27, 128, 128], replicated
The draws below stay inside these ranges and needn't reach their ends.
Inputs may be any that keep to these rules, and one draw needn't show every extreme that they name: Entries name only live slots; slots at or above a column's count have no neighbours; the relation is symmetric: if slot s of column (i, j) names slot t in direction d, then slot t of column (i+dx, j+dy) names s in the opposite direction, and the blocks are adjacent in space; columns outside the grid are never named. `counts`: some column of every workpiece has 4 live slots.
All inputs are finite; a program needn't handle non-finite values.
Results may differ from the reference program's by a relative error of at most 0.012.
Values may be sent and summed in bfloat16 or wider, within the bound.
A program may use at most 192 MiB of HBM per device.

```python
import jax
import jax.numpy as jnp
from jax import lax

C = 128
BE = 8
NB = 4
BATCH = 2
COLS_X = 4
COLS_Y = 4
XV = 32
YV = 32


def column_layout(key):
    height_key = jax.random.fold_in(key, 7)
    count_key = jax.random.fold_in(key, 11)
    chosen_key = jax.random.fold_in(key, 13)
    heights = jax.random.randint(height_key, (BATCH, COLS_X, COLS_Y), 0, 2)
    drawn = jax.random.randint(count_key, (BATCH, COLS_X * COLS_Y), 1, NB + 1)
    chosen = jax.random.randint(chosen_key, (BATCH,), 0, COLS_X * COLS_Y)
    forced = jnp.arange(COLS_X * COLS_Y)[None, :] == chosen[:, None]
    counts = jnp.where(forced, NB, drawn).reshape(BATCH, COLS_X, COLS_Y)
    return (heights.astype(jnp.int32), counts.astype(jnp.int32))


def draw_counts(key, part):
    heights, counts = column_layout(key)
    return counts


def draw_neighbours(key, part):
    heights, counts = column_layout(key)
    slot_ids = jnp.arange(NB, dtype=jnp.int32)
    height_pad = jnp.pad(heights, ((0, 0), (1, 1), (1, 1)))
    count_pad = jnp.pad(counts, ((0, 0), (1, 1), (1, 1)))
    entries = []
    for shift_x in range(3):
        for shift_y in range(3):
            for shift_z in range(3):
                if shift_x * 9 + shift_y * 3 + shift_z == 13:
                    continue
                near_height = height_pad[:, shift_x:shift_x + COLS_X, shift_y:shift_y + COLS_Y]
                near_count = count_pad[:, shift_x:shift_x + COLS_X, shift_y:shift_y + COLS_Y]
                target = heights[..., None] + slot_ids + (shift_z - 1) - near_height[..., None]
                valid = (target >= 0) & (target < near_count[..., None]) & (slot_ids < counts[..., None])
                entries.append(jnp.where(valid, target, -1))
    return jnp.stack(entries, axis=-1).astype(jnp.int32)


def shard_levels(rng, extent, cuts, least, top_value):
    def one(axis_at, parts):
        steps = jax.random.uniform(jax.random.fold_in(jax.random.fold_in(rng, 6), axis_at), (parts,), jnp.float32, least / len(cuts), top_value / len(cuts))
        return jnp.repeat(jnp.exp(steps), extent[axis_at] // parts).reshape((-1,) + (1,) * (len(extent) - axis_at - 1))

    level = one(*cuts[0])
    for cut in cuts[1:]:
        level = level * one(*cut)
    return level


def normal_values(key, shape, scale, limit, split=(), kind=jnp.bfloat16):
    gain = shard_levels(key, shape, split, -0.22, 0.18) if split else 1.0
    values = jax.random.normal(key, shape, jnp.float32) * scale * gain
    return jnp.minimum(jnp.maximum(values, -limit), limit).astype(kind)


def setup_inputs(seed: int = 0) -> dict:
    streams_of = jax.random.split(jax.random.key(seed), 7)
    return {
        "features": normal_values(streams_of[0], (BATCH, XV, YV, NB, BE, C), 1.0, 6.0, ((0, 2), (1, 4), (2, 4))),
        "cotangent": normal_values(streams_of[1], (BATCH, XV, YV, NB, BE, C), 1.0, 6.0, ((0, 2), (1, 4), (2, 4))),
        "first_weight": normal_values(streams_of[2], (27, C, C), (27 * C) ** -0.5, 0.109375),
        "second_weight": normal_values(streams_of[3], (27, C, C), (27 * C) ** -0.5, 0.109375),
        "neighbours": draw_neighbours(jax.random.fold_in(streams_of[6], 71), 0),
        "counts": draw_counts(jax.random.fold_in(streams_of[6], 71), 0),
    }


def padded_blocks(halo_field, neighbour):
    block_edge = halo_field.shape[0] - 2
    ranges_xy = [(0, 1), (1, block_edge + 1), (block_edge + 1, block_edge + 2)]
    ranges_z = [(block_edge - 1, block_edge), (0, block_edge), (0, 1)]
    planes = []
    for shift_x in range(3):
        row_list = []
        for shift_y in range(3):
            slab_list = []
            for shift_z in range(3):
                direction = shift_x * 9 + shift_y * 3 + shift_z
                low_x, high_x = ranges_xy[shift_x]
                low_y, high_y = ranges_xy[shift_y]
                low_z, high_z = ranges_z[shift_z]
                region = halo_field[low_x:high_x, low_y:high_y, :, low_z:high_z]
                if direction == 13:
                    slab_piece = region
                else:
                    entry = direction if direction < 13 else direction - 1
                    target = neighbour[:, entry]
                    valid = (target >= 0).astype(region.dtype)[None, None, :, None, None]
                    slab_piece = jnp.take(region, jnp.maximum(target, 0), axis=2) * valid
                slab_list.append(slab_piece)
            row_list.append(jnp.concatenate(slab_list, axis=3))
        planes.append(jnp.concatenate(row_list, axis=1))
    return jnp.concatenate(planes, axis=0)


def patch_matrix(padded, block_edge):
    pieces = []
    for shift_x in range(3):
        for shift_y in range(3):
            for shift_z in range(3):
                pieces.append(padded[shift_x:shift_x + block_edge, shift_y:shift_y + block_edge, :, shift_z:shift_z + block_edge])
    stacked = jnp.concatenate(pieces, axis=-1)
    return stacked.reshape(-1, stacked.shape[-1])


def flipped_weight(weight):
    return jnp.transpose(weight[::-1], (0, 2, 1))


def silu_slope(values):
    logistic = jax.nn.sigmoid(values)
    return logistic * (1.0 + values * (1.0 - logistic))


def column_start(column_x, column_y):
    zero_index = jnp.zeros((), jnp.int32)
    start_x = (column_x * BE).astype(jnp.int32)
    start_y = (column_y * BE).astype(jnp.int32)
    return (start_x, start_y, zero_index, zero_index, zero_index)


def column_patches(padded_field, neighbours_w, column_id):
    column_x = (column_id // COLS_Y).astype(jnp.int32)
    column_y = (column_id % COLS_Y).astype(jnp.int32)
    halo_field = lax.dynamic_slice(padded_field, column_start(column_x, column_y), (BE + 2, BE + 2, NB, BE, C))
    return patch_matrix(padded_blocks(halo_field, neighbours_w[column_x, column_y]), BE)


def pad_field(field):
    return jnp.pad(field, ((1, 1), (1, 1), (0, 0), (0, 0), (0, 0)))


def convolve_field(field, neighbours_w, weight):
    padded_field = pad_field(field)
    matrix = weight.reshape(27 * C, C)

    def per_column(column_id):
        columns = column_patches(padded_field, neighbours_w, column_id)
        return jnp.dot(columns, matrix, preferred_element_type=jnp.float32).reshape(BE, BE, NB, BE, C)

    result = lax.map(per_column, jnp.arange(COLS_X * COLS_Y, dtype=jnp.int32))
    result = result.reshape(COLS_X, COLS_Y, BE, BE, NB, BE, C)
    return jnp.transpose(result, (0, 2, 1, 3, 4, 5, 6)).reshape(XV, YV, NB, BE, C)


def weight_grad_field(field, grad_field, neighbours_w):
    padded_field = pad_field(field)

    def advance(running, column_id):
        columns = column_patches(padded_field, neighbours_w, column_id)
        column_x = (column_id // COLS_Y).astype(jnp.int32)
        column_y = (column_id % COLS_Y).astype(jnp.int32)
        grads = lax.dynamic_slice(grad_field, column_start(column_x, column_y), (BE, BE, NB, BE, C)).reshape(-1, C)
        term = lax.dot_general(columns, grads, (((0,), (0,)), ((), ())), preferred_element_type=jnp.float32)
        return running + term, None

    running, unused = lax.scan(advance, jnp.zeros((27 * C, C), jnp.float32), jnp.arange(COLS_X * COLS_Y, dtype=jnp.int32))
    return running.reshape(27, C, C)


def live_field(counts_w):
    live_mask = (jnp.arange(NB, dtype=jnp.int32)[None, None, :] < counts_w[:, :, None]).astype(jnp.float32)
    live_mask = jnp.repeat(jnp.repeat(live_mask, BE, axis=0), BE, axis=1)
    return live_mask[:, :, :, None, None]


def reference(features, cotangent, first_weight, second_weight, neighbours, counts):
    grad_scale = float(BATCH * COLS_X * COLS_Y * NB * BE ** 3) ** -0.5
    flip_first = flipped_weight(first_weight)
    flip_second = flipped_weight(second_weight)
    outputs = []
    input_grads = []
    first_total = jnp.zeros((27, C, C), jnp.float32)
    second_total = jnp.zeros((27, C, C), jnp.float32)
    for member in range(BATCH):
        live_mask = live_field(counts[member])
        links = neighbours[member]
        masked = features[member] * live_mask.astype(features.dtype)
        pre_first = convolve_field(masked, links, first_weight)
        hidden = (jax.nn.silu(pre_first) * live_mask).astype(jnp.bfloat16)
        pre_second = convolve_field(hidden, links, second_weight)
        summed = masked.astype(jnp.float32) + pre_second
        outputs.append((jax.nn.silu(summed) * live_mask).astype(jnp.bfloat16))
        back_second = (cotangent[member].astype(jnp.float32) * silu_slope(summed) * live_mask).astype(jnp.bfloat16)
        second_total = second_total + weight_grad_field(hidden, back_second, links)
        back_hidden = convolve_field(back_second, links, flip_second)
        back_first = (back_hidden * silu_slope(pre_first) * live_mask).astype(jnp.bfloat16)
        first_total = first_total + weight_grad_field(masked, back_first, links)
        back_input = convolve_field(back_first, links, flip_first)
        input_grads.append(((back_second.astype(jnp.float32) + back_input) * live_mask).astype(jnp.bfloat16))
    return (jnp.stack(outputs), jnp.stack(input_grads), first_total * grad_scale, second_total * grad_scale)
```

```python
import functools

import jax
import jax.numpy as jnp
from jax import lax
from jax.experimental import pallas as pl
from jax.experimental.pallas import tpu as pltpu
from jax.sharding import PartitionSpec as P

DIRS = [(dx, dy) for dx in (-1, 0, 1) for dy in (-1, 0, 1) if (dx, dy) != (0, 0)]
F32 = jnp.float32
BF16 = jnp.bfloat16
UNIT = 16


def slope(v):
    s = jax.nn.sigmoid(v)
    return s * (1.0 + v * (1.0 - s))


MODES = (("abz", False), ("yz", True))


def side_of(ny):
    f = 1
    while f * f < ny:
        f += 1
    return f if f * f == ny else None


def layout(nx, ny, nd, ch):
    n = nx * ny
    per = 9 * ch // UNIT
    total = -(-3 * per // (n * nd))
    pieces = []
    sems = 0
    room = 0
    for g in range(2):
        mode, whole = MODES[g]
        f = side_of(ny)
        sizes = (f, f, nx) if mode == "abz" and f else (ny, nx)
        done = 0
        for b in range(3):
            upto = total if b == 2 else min((b + 1) * per // (n * nd), total)
            q = upto - done
            if q <= 0:
                continue
            item = dict(g=g, b=b, q=q, base=done * n * nd, sizes=sizes, whole=whole, rs=[], ag=[], slot=[])
            item["pair"] = sems
            sems += 1
            left = n * q
            for l, s in enumerate(sizes):
                last = whole and l == len(sizes) - 1
                step = left if last else left // s
                item["rs"].append(sems)
                sems += s
                item["ag"].append(sems)
                sems += 0 if last else s
                item["slot"].append((room, step))
                room += s * step
                left = left // s
            item["fw"] = sems
            sems += sizes[0]
            pieces.append(item)
            done = upto
    return pieces, sems, room, total * n * nd


def kernel(
    nx,
    ny,
    nd,
    feat,
    cot,
    w1,
    w2,
    nb,
    count,
    out_ref,
    gin_ref,
    gw1_ref,
    gw2_ref,
    fld,
    rx,
    ry,
    rc,
    pc_a,
    pc_b,
    pc_c,
    pre,
    gt,
    send_sem,
    recv_sem,
    w1f,
    w2f,
    sel,
    live,
    gb,
    dx_buf,
    hs,
    rb,
    fin,
    sum_send,
    sum_recv,
):
    edge = feat.shape[0]
    rows = feat.shape[2]
    ch = feat.shape[3]
    pairs = edge // 2
    plane = edge * rows
    ix = lax.axis_index("sx")
    iy = lax.axis_index("sy")

    def there(dx, dy):
        ok = None
        for d, i, n in ((dx, ix, nx), (dy, iy, ny)):
            if d == 0:
                continue
            c = (i < n - 1) if d > 0 else (i > 0)
            ok = c if ok is None else jnp.logical_and(ok, c)
        return ok

    def peer(dx, dy):
        px = jnp.minimum(jnp.maximum(ix + dx, 0), nx - 1)
        py = jnp.minimum(jnp.maximum(iy + dy, 0), ny - 1)
        return {"sx": px, "sy": py}

    def halo_ref(f, dx, dy):
        if dy == 0:
            return rx.at[f, (dx + 1) // 2]
        if dx == 0:
            return ry.at[f, (dy + 1) // 2]
        return rc.at[f, (dx + 1) // 2 * 2 + (dy + 1) // 2]

    def desc(f, k):
        dx, dy = DIRS[k]
        far_x = edge - 1 if dx > 0 else 0
        far_y = edge - 1 if dy > 0 else 0
        if dy == 0:
            src = fld.at[f, far_x]
        elif dx == 0:
            src = fld.at[f, :, far_y]
        else:
            src = fld.at[f, far_x, far_y]
        return pltpu.make_async_remote_copy(
            src_ref=src,
            dst_ref=halo_ref(f, -dx, -dy),
            send_sem=send_sem.at[f, k],
            recv_sem=recv_sem.at[f, k],
            device_id=peer(dx, dy),
            device_id_type=pl.DeviceIdType.MESH,
        )

    def send(f):
        for k, (dx, dy) in enumerate(DIRS):
            @pl.when(there(dx, dy))
            def _(k=k):
                desc(f, k).start()

    def arrive(f):
        for k, (dx, dy) in enumerate(DIRS):
            @pl.when(there(-dx, -dy))
            def _(k=k):
                desc(f, k).wait_recv()

    def drain(f):
        for k, (dx, dy) in enumerate(DIRS):
            @pl.when(there(dx, dy))
            def _(k=k):
                desc(f, k).wait_send()

    def put(pc, x, yp, tile):
        t = tile.astype(BF16)
        for b in range(3):
            y = yp - b
            if 0 <= y < edge:
                for c in range(3):
                    lo = (b * 3 + c) * ch
                    pc[x, y, :, lo : lo + ch] = t[c * rows : (c + 1) * rows]

    def line(pc, x, s, tiles):
        cat = jnp.concatenate(tiles, axis=1)
        got = jnp.dot(s, cat, preferred_element_type=F32)
        for y in range(edge):
            put(pc, x, y + 1, got[:, y * ch : (y + 1) * ch])

    def inner(f, pc):
        def body(x, carry):
            line(pc, x + 1, sel[4], [fld[f, x, y] for y in range(edge)])
            return carry

        lax.fori_loop(0, edge, body, 0)

    def outer(f, pc):
        for h in range(2):
            x = 0 if h == 0 else edge + 1
            line(pc, x, sel[6 * h + 1], [rx[f, h, y] for y in range(edge)])
            for g in range(2):
                yp = 0 if g == 0 else edge + 1
                put(pc, x, yp, jnp.dot(sel[6 * h + 2 * g], rc[f, h * 2 + g], preferred_element_type=F32))
            cat = jnp.concatenate([ry[f, h, x] for x in range(edge)], axis=1)
            got = jnp.dot(sel[3 + 2 * h], cat, preferred_element_type=F32)
            for x in range(edge):
                put(pc, x + 1, 0 if h == 0 else edge + 1, got[:, x * ch : (x + 1) * ch])

    def conv(pc, w, use, hooks=None):
        def body(i, carry):
            left = None
            right = None
            for p in range(4):
                lhs = pc[2 * i + p].reshape(plane, 9 * ch)
                wl = w[9 * p : 9 * p + 9].reshape(9 * ch, ch) if p < 3 else None
                wr = w[9 * p - 9 : 9 * p].reshape(9 * ch, ch) if p > 0 else None
                if wr is None:
                    left = jnp.dot(lhs, wl, preferred_element_type=F32)
                elif wl is None:
                    right = right + jnp.dot(lhs, wr, preferred_element_type=F32)
                else:
                    both = jnp.dot(lhs, jnp.concatenate([wl, wr], axis=1), preferred_element_type=F32)
                    left = left + both[:, :ch]
                    right = both[:, ch:] if right is None else right + both[:, ch:]
            use(i, 0, left)
            use(i, 1, right)
            hooked(i, hooks)
            return carry

        lax.fori_loop(0, pairs, body, 0)

    def keep_t(i, h, v):
        gt[h * ch : (h + 1) * ch, pl.ds(pl.multiple_of(i * plane, plane), plane)] = v.T.astype(BF16)

    def tap_out(g, a, b, v):
        per = ch // UNIT
        for c in range(3):
            t = v[:, c * ch : (c + 1) * ch].T.astype(BF16).reshape(per, UNIT, ch)
            gb[g, pl.ds(((b * 3 + a) * 3 + c) * per, per)] = t

    def hooked(i, hooks):
        for at, fns in sorted((hooks or {}).items()):
            @pl.when(i == at)
            def _(fns=fns):
                for fn in fns:
                    fn()

    def wgrad(pc, g, hooks):
        def body(b, carry):
            lanes = pl.ds(pl.multiple_of(b * (3 * ch), 3 * ch), 3 * ch)
            part = None
            for p in range(4):
                acc = None
                for i in range(pairs):
                    rhs = pc[2 * i + p, :, :, lanes].reshape(plane, 3 * ch)
                    lhs = gt[:, i * plane : (i + 1) * plane]
                    if p == 0:
                        lhs = lhs[:ch]
                    elif p == 3:
                        lhs = lhs[ch:]
                    t = jnp.dot(lhs, rhs, preferred_element_type=F32)
                    acc = t if acc is None else acc + t
                if p == 3:
                    tap_out(g, 2, b, part + acc)
                elif p > 0:
                    tap_out(g, p - 1, b, part + acc[ch:])
                if p < 3:
                    part = acc[:ch]
            hooked(b, hooks)
            return carry

        lax.fori_loop(0, 3, body, 0)

    n = nx * ny
    core = lax.axis_index("dp")
    me = ix * ny + iy
    mesh_id = pl.DeviceIdType.MESH
    pieces, _, _, units = layout(nx, ny, nd, ch)
    side = side_of(ny)

    def each(lo, hi, fn):
        if hi - lo <= 3:
            for o in range(lo, hi):
                fn(o)
            return

        def body(o, carry):
            fn(o)
            return carry

        lax.fori_loop(lo, hi, body, 0)

    def group(p):
        return {"sx": p // ny, "sy": lax.rem(p, ny)}

    class Sum:
        def __init__(self, item):
            self.it = item
            self.g = item["g"]
            q = item["q"]
            self.sizes = item["sizes"]
            m = self.m = len(self.sizes)
            if m == 3:
                cx = lax.rem(iy, side)
                cy = lax.div(iy, side)
                first = cx + core * (cy - cx)
                second = cx + cy - first
                self.coords = (first, second, ix)
                self.other = second
                self.steps = (1 + core * (side - 1), side - core * (side - 1))
            else:
                self.coords = (iy, ix)
                self.other = iy
                self.steps = (1,)
            self.size = [n * q]
            self.off = [0]
            for l in range(m):
                self.size.append(self.size[-1] // self.sizes[l])
                self.off.append(self.off[-1] + self.coords[l] * self.size[-1])
            self.hb = item["base"] // nd
            self.mine = item["base"] + core * (n * q)
            self.theirs = item["base"] + (1 - core) * (n * q)
            self.whole = item["whole"]

        def to(self, l, o):
            c = self.coords[l]
            p = lax.rem(c + o, self.sizes[l])
            if l == self.m - 1:
                return p, {"sx": p}
            return p, {"sy": iy + (p - c) * self.steps[l]}

        def frm(self, l, o):
            return lax.rem(self.coords[l] + self.sizes[l] - o, self.sizes[l])

        def copy(self, src, dst, k, dev):
            return pltpu.make_async_remote_copy(
                src_ref=src,
                dst_ref=dst,
                send_sem=sum_send.at[k],
                recv_sem=sum_recv.at[k],
                device_id=dev,
                device_id_type=mesh_id,
            )

        def pair(self):
            return self.copy(
                gb.at[self.g, pl.ds(self.theirs, self.size[0])],
                dx_buf.at[self.g, pl.ds(self.hb, self.size[0])],
                self.it["pair"],
                {"dp": 1 - core},
            )

        def last(self, l):
            return self.whole and l == self.m - 1

        def rs(self, l, o):
            p, dev = self.to(l, o)
            room, step = self.it["slot"][l]
            at = self.off[l] if self.last(l) else self.off[l] + p * step
            return self.copy(
                hs.at[self.g, pl.ds(self.hb + at, step)],
                rb.at[pl.ds(room + o * step, step)],
                self.it["rs"][l] + o,
                dev,
            )

        def ag(self, l, o, owner):
            _, dev = self.to(l, o)
            size = self.size[l + 1]
            here = pl.ds(self.mine + self.off[l] + owner * size, size)
            return self.copy(fin.at[self.g, here], fin.at[self.g, here], self.it["ag"][l] + o, dev)

        def fw(self, o, base, c):
            size = self.size[1]
            here = pl.ds(base + lax.rem(c + self.sizes[0] - o, self.sizes[0]) * size, size)
            return self.copy(fin.at[self.g, here], fin.at[self.g, here], self.it["fw"] + o, {"dp": 1 - core})

        def begin(self):
            self.pair().start()

        def total(self, l, at, size):
            own = hs[self.g, pl.ds(self.hb + at, size)] if l >= 0 else gb[self.g, pl.ds(self.mine + at, size)]
            v = own.astype(F32)
            if l < 0:
                return v + dx_buf[self.g, pl.ds(self.hb + at, size)].astype(F32)
            room, step = self.it["slot"][l]
            back = at - self.off[l + 1]

            def add(o, acc):
                return acc + rb[pl.ds(room + o * step + back, size)].astype(F32)

            if self.sizes[l] <= 4:
                for o in range(1, self.sizes[l]):
                    v = add(o, v)
                return v
            return lax.fori_loop(1, self.sizes[l], add, v)

        def reduce(self, l):
            if l < 0:
                self.pair().wait_recv()
            else:
                each(1, self.sizes[l], lambda o: self.rs(l, o).wait_recv())
            nxt = l + 1
            if nxt == self.m:
                size = self.size[self.m]
                v = self.total(l, self.off[self.m], size)
                fin[self.g, pl.ds(self.mine + self.off[self.m], size)] = v.astype(BF16)
                self.share(l)
                return
            room, step = self.it["slot"][nxt]
            if self.last(nxt):
                v = self.total(l, self.off[nxt], step).astype(BF16)
                hs[self.g, pl.ds(self.hb + self.off[nxt], step)] = v
                rb[pl.ds(room, step)] = v
                each(1, self.sizes[nxt], lambda o: self.rs(nxt, o).start())
                return

            def one(o):
                at = self.off[nxt] + lax.rem(self.coords[nxt] + o, self.sizes[nxt]) * step
                hs[self.g, pl.ds(self.hb + at, step)] = self.total(l, at, step).astype(BF16)

            def go(o):
                one(o)
                self.rs(nxt, o).start()

            each(1, self.sizes[nxt], go)
            one(0)

        def settle(self):
            l = self.m - 1
            each(1, self.sizes[l], lambda o: self.rs(l, o).wait_recv())
            room, step = self.it["slot"][l]

            def part(p):
                return rb[pl.ds(room + self.frm(l, p) * step, step)].astype(F32)

            v = part(0)
            if self.sizes[l] <= 4:
                for p in range(1, self.sizes[l]):
                    v = v + part(p)
            else:
                v = lax.fori_loop(1, self.sizes[l], lambda p, acc: acc + part(p), v)
            fin[self.g, pl.ds(self.mine + self.off[l], step)] = v.astype(BF16)
            self.share(l - 1)

        def share(self, l):
            each(1, self.sizes[l], lambda o: self.ag(l, o, self.coords[l]).start())
            if l == 0:
                self.fw(0, self.mine, self.coords[0]).start()

        def gather(self, l):
            def one(o):
                self.ag(l, o, self.frm(l, o)).wait_recv()
                if l == 0:
                    self.fw(o, self.mine, self.coords[0]).start()

            each(1, self.sizes[l], one)
            if l > 0:
                self.share(l - 1)

        def arrive(self):
            each(0, self.sizes[0], lambda o: self.fw(o, self.theirs, self.other).wait_recv())

        def stages(self):
            out = [self.begin]
            for l in range(-1, self.m - (1 if self.whole else 0)):
                out.append(functools.partial(self.reduce, l))
            if self.whole:
                out.append(self.settle)
            for l in reversed(range(self.m - (1 if self.whole else 0))):
                out.append(functools.partial(self.gather, l))
            out.append(self.arrive)
            return out

        def drain(self):
            self.pair().wait_send()
            for l in range(self.m):
                each(1, self.sizes[l], lambda o: self.rs(l, o).wait_send())
                if not self.last(l):
                    each(1, self.sizes[l], lambda o: self.ag(l, o, self.coords[l]).wait_send())
            each(0, self.sizes[0], lambda o: self.fw(o, self.mine, self.coords[0]).wait_send())

    sums = [Sum(item) for item in pieces]
    queue = {(s.g, s.it["b"]): s.stages() for s in sums}

    listed = set()

    def adv(g, b, s):
        listed.add((g, b, s))

        def run():
            if s < len(queue.get((g, b), [])):
                queue[g, b][s]()

        return run

    def finish(g, ref):
        per = ch // UNIT
        for k in range(27):
            a, b, c = k // 9, k // 3 % 3, k % 3
            j = (b * 3 + a) * 3 + c
            ref[k * per : (k + 1) * per] = fin[g, j * per : (j + 1) * per]

    for dx, dy in DIRS:
        @pl.when(jnp.logical_not(there(dx, dy)))
        def _(dx=dx, dy=dy):
            for f in range(4):
                r = halo_ref(f, dx, dy)
                r[...] = jnp.zeros(r.shape, BF16)

    barrier = pltpu.get_barrier_semaphore()
    each(
        1,
        n,
        lambda o: pl.semaphore_signal(
            barrier, inc=1, device_id=group(lax.rem(me + o, n)), device_id_type=mesh_id
        ),
    )
    pl.semaphore_signal(barrier, inc=1, device_id={"dp": 1 - core}, device_id_type=mesh_id)

    spare = units - 27 * (ch // UNIT)
    if spare:
        for g in range(2):
            gb[g, units - spare :] = jnp.zeros((spare, UNIT, ch), BF16)

    slots = rows // edge
    row = lax.broadcasted_iota(jnp.int32, (plane, ch), 0)
    live[...] = jnp.where(lax.rem(lax.div(row, edge), slots) < count[0], 1.0, 0.0).astype(F32)

    r = lax.broadcasted_iota(jnp.int32, (3 * rows, rows), 0)
    col = lax.broadcasted_iota(jnp.int32, (3 * rows, rows), 1)
    src = lax.rem(r, edge) + lax.div(r, rows) - 1
    dz = jnp.where(src < 0, 0, jnp.where(src >= edge, 2, 1))
    key = dz * slots + lax.rem(lax.div(r, edge), slots)
    same_z = lax.rem(src + edge, edge) == lax.rem(col, edge)
    slot = lax.div(col, edge)
    for d in range(9):
        target = jnp.full((3 * rows, rows), -1, jnp.int32)
        for k in range(3):
            way = d * 3 + k
            for sl in range(slots):
                name = sl if way == 13 else nb[sl, way if way < 13 else way - 1]
                target = jnp.where(key == k * slots + sl, name, target)
        hit = jnp.logical_and(same_z, target == slot)
        sel[d] = jnp.where(hit, 1.0, 0.0).astype(F32).astype(BF16)

    def flip(w, to):
        def body(k, carry):
            to[k] = w[26 - k].astype(F32).T.astype(BF16)
            return carry

        lax.fori_loop(0, 27, body, 0)

    def mask_in(x, carry):
        v = feat[x].astype(F32).reshape(plane, ch) * live[...]
        fld[0, x] = v.astype(BF16).reshape(edge, rows, ch)
        return carry

    lax.fori_loop(0, edge, mask_in, 0)

    pl.semaphore_wait(barrier, n)

    def store(f, x, v):
        fld[f, x] = v.astype(BF16).reshape(edge, rows, ch)

    send(0)
    inner(0, pc_a)
    flip(w2, w2f)
    arrive(0)
    outer(0, pc_a)

    def use1(i, h, v):
        x = 2 * i + h
        pre[x] = v
        store(1, x, v * jax.nn.sigmoid(v) * live[...])

    conv(pc_a, w1, use1)
    send(1)
    inner(1, pc_b)
    flip(w1, w1f)
    arrive(1)
    outer(1, pc_b)

    def use2(i, h, v):
        x = 2 * i + h
        v = v + fld[0, x].reshape(plane, ch).astype(F32)
        s = jax.nn.sigmoid(v)
        out_ref[x] = (v * s * live[...]).astype(BF16).reshape(edge, rows, ch)
        g = cot[x].reshape(plane, ch).astype(F32) * (s * (1.0 + v * (1.0 - s))) * live[...]
        store(2, x, g)
        keep_t(i, h, g)

    AT = {
        "w2": {0: [adv(0, 0, 0)], 1: [adv(0, 1, 0), adv(0, 0, 1)], 2: [adv(0, 2, 0), adv(0, 1, 1)]},
        "o2": [adv(0, 2, 1)],
        "c3": {
            0: [adv(0, 0, 2)],
            1: [adv(0, 1, 2)],
            2: [adv(0, 2, 2), adv(0, 0, 3)],
            3: [adv(0, 1, 3)],
        },
        "w1": {
            0: [adv(1, 0, 0), adv(0, 2, 3)],
            1: [adv(1, 1, 0), adv(1, 0, 1), adv(0, 0, 4), adv(0, 1, 4)],
            2: [adv(1, 2, 0), adv(1, 1, 1), adv(0, 2, 4)],
        },
        "o3": [adv(1, 2, 1), adv(1, 0, 2)],
        "c4": {
            0: [adv(1, 1, 2), adv(0, 0, 5)],
            1: [adv(1, 2, 2), adv(0, 1, 5)],
            2: [adv(0, 2, 5), adv(0, 0, 6), adv(1, 0, 3)],
            3: [adv(0, 1, 6), adv(0, 2, 6), adv(1, 1, 3)],
        },
        "end": [adv(0, 0, 7), adv(0, 1, 7), adv(1, 2, 3), adv(1, 0, 4), adv(0, 2, 7), adv(1, 1, 4), adv(0, 0, 8), adv(1, 2, 4)],
    }

    conv(pc_b, w2, use2)
    send(2)
    inner(2, pc_c)
    wgrad(pc_b, 0, AT["w2"])
    arrive(2)
    outer(2, pc_c)
    for fn in AT["o2"]:
        fn()

    def use3(i, h, v):
        x = 2 * i + h
        g = v * slope(pre[x]) * live[...]
        store(3, x, g)
        keep_t(i, h, g)

    conv(pc_c, w2f, use3, AT["c3"])
    send(3)
    wgrad(pc_a, 1, AT["w1"])
    inner(3, pc_c)
    arrive(3)
    outer(3, pc_c)
    for fn in AT["o3"]:
        fn()

    def use4(i, h, v):
        x = 2 * i + h
        g = (fld[2, x].reshape(plane, ch).astype(F32) + v) * live[...]
        gin_ref[x] = g.astype(BF16).reshape(edge, rows, ch)

    conv(pc_c, w1f, use4, AT["c4"])
    for fn in AT["end"]:
        fn()
    for k, todo in queue.items():
        for s, fn in enumerate(todo):
            if k + (s,) not in listed:
                fn()
    finish(0, gw2_ref)
    finish(1, gw1_ref)
    for f in range(4):
        drain(f)
    for s in sums:
        s.drain()


def shards(nx, ny, nd, features, cotangent, first_weight, second_weight, neighbours, counts):
    _, edge, _, slots, _, ch = features.shape
    rows = slots * edge
    plane = edge * rows
    flat = (edge, edge, rows, ch)
    scale = float(nx * ny * nd * slots * edge**3) ** -0.5
    vmem = pl.BlockSpec(memory_space=pltpu.VMEM)
    smem = pl.BlockSpec(memory_space=pltpu.SMEM)
    _, nsem, room, units = layout(nx, ny, nd, ch)
    gshape = jax.ShapeDtypeStruct((units, UNIT, ch), BF16)
    fshape = jax.ShapeDtypeStruct(flat, BF16)
    out, gin, g1, g2 = pl.pallas_call(
        functools.partial(kernel, nx, ny, nd),
        out_shape=[fshape, fshape, gshape, gshape],
        in_specs=[vmem] * 4 + [smem] * 2,
        out_specs=[vmem] * 4,
        scratch_shapes=[
            pltpu.VMEM((4,) + flat, BF16),
            pltpu.VMEM((4, 2, edge, rows, ch), BF16),
            pltpu.VMEM((4, 2, edge, rows, ch), BF16),
            pltpu.VMEM((4, 4, rows, ch), BF16),
            pltpu.VMEM((edge + 2, edge, rows, 9 * ch), BF16),
            pltpu.VMEM((edge + 2, edge, rows, 9 * ch), BF16),
            pltpu.VMEM((edge + 2, edge, rows, 9 * ch), BF16),
            pltpu.VMEM((edge, plane, ch), F32),
            pltpu.VMEM((2 * ch, edge // 2 * plane), BF16),
            pltpu.SemaphoreType.DMA((4, len(DIRS))),
            pltpu.SemaphoreType.DMA((4, len(DIRS))),
            pltpu.VMEM((27, ch, ch), BF16),
            pltpu.VMEM((27, ch, ch), BF16),
            pltpu.VMEM((9, 3 * rows, rows), BF16),
            pltpu.VMEM((plane, ch), F32),
            pltpu.VMEM((2, units, UNIT, ch), BF16),
            pltpu.VMEM((2, units // nd, UNIT, ch), BF16),
            pltpu.VMEM((2, units // nd, UNIT, ch), BF16),
            pltpu.VMEM((room, UNIT, ch), BF16),
            pltpu.VMEM((2, units, UNIT, ch), BF16),
            pltpu.SemaphoreType.DMA((nsem,)),
            pltpu.SemaphoreType.DMA((nsem,)),
        ],
        compiler_params=pltpu.CompilerParams(
            collective_id=0, has_side_effects=True, vmem_limit_bytes=60 * 1024 * 1024
        ),
    )(
        features.reshape(flat),
        cotangent.reshape(flat),
        first_weight,
        second_weight,
        neighbours[0, 0, 0],
        counts.reshape(1),
    )
    def finish(g):
        g = g.reshape(-1, ch)[: 27 * ch]
        return g.reshape(27, ch, ch).astype(F32) * scale

    return out.reshape(features.shape), gin.reshape(features.shape), finish(g1), finish(g2)


def solution(mesh):
    field = P("dp", "sx", "sy", None, None, None)
    return jax.shard_map(
        functools.partial(shards, mesh.shape["sx"], mesh.shape["sy"], mesh.shape["dp"]),
        mesh=mesh,
        in_specs=(field, field, P(), P(), P("dp", "sx", "sy", None, None), P("dp", "sx", "sy")),
        out_specs=(field, field, P(), P()),
        check_vma=False,
    )
```

```python
import functools

import jax
import jax.numpy as jnp
from jax import lax
from jax.experimental import pallas as pl
from jax.experimental.pallas import tpu as pltpu
from jax.sharding import PartitionSpec as P

DIRS = [(dx, dy) for dx in (-1, 0, 1) for dy in (-1, 0, 1) if (dx, dy) != (0, 0)]
F32 = jnp.float32
BF16 = jnp.bfloat16
UNIT = 16


def slope(v):
    s = jax.nn.sigmoid(v)
    return s * (1.0 + v * (1.0 - s))


MODES = (
    ("yz", "yz", "yz", "yz", "yz"),
    ("yz", "yz", "yzw", "yzw", "yzw"),
)
STEPS = {
    (0, 0): ("w2.0", "w2.2", "c3.3", "w1.4", "c4.2",),
    (0, 1): ("w2.1", "w2.3", "c3.3", "w1.4", "c4.2",),
    (0, 2): ("w2.2", "w2.4", "c3.3", "w1.4", "c4.2",),
    (0, 3): ("w2.3", "o2", "w1.0", "o3", "c4.2",),
    (0, 4): ("w2.4", "c3.0", "w1.1", "o3", "c4.2",),
    (1, 0): ("w1.0", "w1.2", "c4.1",),
    (1, 1): ("w1.1", "w1.3", "c4.1",),
    (1, 2): ("w1.2", "w1.4", "c4.1",),
    (1, 3): ("w1.3", "o3", "c4.3",),
    (1, 4): ("w1.4", "o3", "c4.3",),
}


def side_of(ny):
    f = 1
    while f * f < ny:
        f += 1
    return f if f * f == ny else None


def layout(nx, ny, nd, ch):
    n = nx * ny
    total = -(-27 * ch // (UNIT * n * nd))
    pieces = []
    sems = 0
    room = 0
    out = {}

    def sent(g, kind, count):
        out[g, kind] = out.get((g, kind), 0) + count

    for g in range(2):
        f = side_of(ny)
        done = 0
        for b in range(5):
            upto = total if b == 4 else min((b + 1) * (6 * ch // UNIT) // (n * nd), total)
            q = upto - done
            if q <= 0:
                continue
            mode = MODES[g][b]
            whole = mode[-1] == "w"
            if mode == "all":
                sizes = (n,)
            elif mode[:3] == "abz" and f:
                sizes = (f, f, nx)
            else:
                sizes = (ny, nx)
            item = dict(g=g, b=b, q=q, base=done * n * nd, sizes=sizes, whole=whole, rs=[], ag=[], slot=[])
            item["pair"] = sems
            sems += 1
            left = n * q
            sent(g, "pair", left)
            for l, s in enumerate(sizes):
                last = whole and l == len(sizes) - 1
                step = left if last else left // s
                item["rs"].append(sems)
                sems += 1
                sent(g, "rs", (s - 1) * step)
                item["ag"].append(sems)
                if l == 0:
                    sems += s
                elif not last:
                    sems += 1
                if not last:
                    sent(g, "ag", (s - 1) * step)
                item["slot"].append((room, step))
                room += s * step
                left = left // s
            item["fw"] = sems
            sems += 1
            sent(g, "fw", n * q)
            pieces.append(item)
            done = upto
    return pieces, sems, room, total * n * nd, out


def kernel(
    nx,
    ny,
    nd,
    feat_in,
    cot_in,
    w1_in,
    w2_in,
    nb,
    count,
    out_hbm,
    gin_hbm,
    gw1_hbm,
    gw2_hbm,
    feat,
    cot,
    w1,
    w2,
    out_ref,
    gin_ref,
    load_sem,
    save_sem,
    fld,
    rx,
    ry,
    rc,
    pc_a,
    pc_b,
    pc_c,
    pre,
    gt,
    send_sem,
    recv_sem,
    w1f,
    w2f,
    sel,
    live,
    gb,
    dx_buf,
    hs,
    rb,
    fin,
    sum_send,
    sum_recv,
):
    edge = feat.shape[0]
    rows = feat.shape[2]
    ch = feat.shape[3]
    pairs = edge // 2
    plane = edge * rows
    ix = lax.axis_index("sx")
    iy = lax.axis_index("sy")

    def there(dx, dy):
        ok = None
        for d, i, n in ((dx, ix, nx), (dy, iy, ny)):
            if d == 0:
                continue
            c = (i < n - 1) if d > 0 else (i > 0)
            ok = c if ok is None else jnp.logical_and(ok, c)
        return ok

    def peer(dx, dy):
        px = jnp.minimum(jnp.maximum(ix + dx, 0), nx - 1)
        py = jnp.minimum(jnp.maximum(iy + dy, 0), ny - 1)
        return {"sx": px, "sy": py}

    def halo_ref(f, dx, dy):
        if dy == 0:
            return rx.at[f, (dx + 1) // 2]
        if dx == 0:
            return ry.at[f, (dy + 1) // 2]
        return rc.at[f, (dx + 1) // 2 * 2 + (dy + 1) // 2]

    late = 2 * (pairs - 2)

    def desc(f, k, part=None):
        dx, dy = DIRS[k]
        far_x = edge - 1 if dx > 0 else 0
        far_y = edge - 1 if dy > 0 else 0
        dst = halo_ref(f, -dx, -dy)
        wait = k
        if dy == 0:
            src = fld.at[f, far_x]
        elif dx == 0:
            src = fld.at[f, :, far_y]
            if part is not None:
                lo, hi = part
                src = fld.at[f, lo:hi, far_y]
                dst = dst.at[lo:hi]
                if lo == late:
                    wait = len(DIRS) + (dy + 1) // 2
        else:
            src = fld.at[f, far_x, far_y]
        return pltpu.make_async_remote_copy(
            src_ref=src,
            dst_ref=dst,
            send_sem=send_sem.at[f, k],
            recv_sem=recv_sem.at[f, wait],
            device_id=peer(dx, dy),
            device_id_type=pl.DeviceIdType.MESH,
        )

    def send(f, keep=lambda dx, dy: True, part=None):
        for k, (dx, dy) in enumerate(DIRS):
            if keep(dx, dy):
                @pl.when(there(dx, dy))
                def _(k=k):
                    desc(f, k, part).start()

    def arrive(f, keep=lambda dx, dy: True):
        for k, (dx, dy) in enumerate(DIRS):
            if keep(dx, dy):
                @pl.when(there(-dx, -dy))
                def _(k=k):
                    desc(f, k).wait_recv()

    def side_y(dx, dy):
        return dx == 0

    def arrive_y(f, part, lo, hi):
        for k, (dx, dy) in enumerate(DIRS):
            if dx == 0:
                @pl.when(there(-dx, -dy))
                def _(k=k, dy=dy):
                    here = halo_ref(f, 0, -dy).at[lo:hi]
                    pltpu.make_async_remote_copy(
                        src_ref=here,
                        dst_ref=here,
                        send_sem=send_sem.at[f, k],
                        recv_sem=recv_sem.at[f, len(DIRS) + (dy + 1) // 2 if part else k],
                        device_id=peer(0, dy),
                        device_id_type=pl.DeviceIdType.MESH,
                    ).wait_recv()

    def drain(f):
        for k, (dx, dy) in enumerate(DIRS):
            @pl.when(there(dx, dy))
            def _(k=k):
                desc(f, k).wait_send()

    def put(pc, x, yp, tile):
        t = tile.astype(BF16)
        for b in range(3):
            y = yp - b
            if 0 <= y < edge:
                for c in range(3):
                    lo = (b * 3 + c) * ch
                    pc[x, y, :, lo : lo + ch] = t[c * rows : (c + 1) * rows]

    def line(pc, x, s, tiles):
        cat = jnp.concatenate(tiles, axis=1)
        got = jnp.dot(s, cat, preferred_element_type=F32)
        for y in range(edge):
            put(pc, x, y + 1, got[:, y * ch : (y + 1) * ch])

    def inner(f, pc):
        def body(x, carry):
            line(pc, x + 1, sel[4], [fld[f, x, y] for y in range(edge)])
            return carry

        lax.fori_loop(0, edge, body, 0)

    def outer_x(f, pc):
        for h in range(2):
            x = 0 if h == 0 else edge + 1
            line(pc, x, sel[6 * h + 1], [rx[f, h, y] for y in range(edge)])
            for g in range(2):
                yp = 0 if g == 0 else edge + 1
                put(pc, x, yp, jnp.dot(sel[6 * h + 2 * g], rc[f, h * 2 + g], preferred_element_type=F32))

    def outer_y(f, pc, xs):
        for h in range(2):
            cat = jnp.concatenate([ry[f, h, x] for x in xs], axis=1)
            got = jnp.dot(sel[3 + 2 * h], cat, preferred_element_type=F32)
            for n_x, x in enumerate(xs):
                put(pc, x + 1, 0 if h == 0 else edge + 1, got[:, n_x * ch : (n_x + 1) * ch])

    def outer(f, pc):
        outer_x(f, pc)
        outer_y(f, pc, range(edge))

    def conv(pc, w, use, hooks=None, turn=0):
        def body(step, carry):
            i = lax.rem(step + turn, pairs) if turn else step

            def lhs(p):
                return pc[2 * i + p].reshape(plane, 9 * ch)

            def tap(a):
                return w[9 * a : 9 * a + 9].reshape(9 * ch, ch)

            low = jnp.concatenate([tap(1), tap(0)], axis=1)
            high = jnp.concatenate([tap(2), tap(1)], axis=1)
            both = jnp.dot(
                jnp.concatenate([lhs(1), lhs(2)], axis=1),
                jnp.concatenate([low, high], axis=0),
                preferred_element_type=F32,
            )
            left = both[:, :ch] + jnp.dot(lhs(0), tap(0), preferred_element_type=F32)
            right = both[:, ch:] + jnp.dot(lhs(3), tap(2), preferred_element_type=F32)
            use(i, 0, left)
            use(i, 1, right)
            hooked(step, hooks)
            return carry

        lax.fori_loop(0, pairs, body, 0)

    def keep_t(i, h, v):
        t = v.T.astype(BF16)
        for a in range(3):
            at = pl.multiple_of((2 * i + h + a) * plane, plane)
            gt[a * ch : (a + 1) * ch, pl.ds(at, plane)] = t

    def tap_out(g, j, wide, v):
        per = ch // UNIT
        for s in range(wide):
            for a in range(3):
                t = v[a][:, s * ch : (s + 1) * ch].T.astype(BF16).reshape(per, UNIT, ch)
                gb[g, pl.ds(((2 * j + s) * 3 + a) * per, per)] = t

    def hooked(i, hooks):
        for at, fns in sorted((hooks or {}).items()):
            @pl.when(i == at)
            def _(fns=fns):
                for fn in fns:
                    fn()

    def taps(pc, g, j, wide):
        lanes = pl.ds(pl.multiple_of(j * (2 * ch), 2 * ch), wide * ch)

        def part(lo, hi, x0, x1):
            rhs = pc[x0:x1, :, :, lanes].reshape((x1 - x0) * plane, wide * ch)
            lhs = gt[lo * ch : hi * ch, x0 * plane : x1 * plane]
            return jnp.dot(lhs, rhs, preferred_element_type=F32)

        mid = part(0, 3, 2, edge)
        low = part(0, 2, 1, 2)
        high = part(1, 3, edge, edge + 1)
        rows3 = (
            mid[:ch] + low[:ch] + part(0, 1, 0, 1),
            mid[ch : 2 * ch] + low[ch:] + high[:ch],
            mid[2 * ch :] + high[ch:] + part(2, 3, edge + 1, edge + 2),
        )
        tap_out(g, j, wide, rows3)

    def wgrad(pc, g, hooks):
        def body(j, carry):
            taps(pc, g, j, 2)
            hooked(j, hooks)
            return carry

        lax.fori_loop(0, 4, body, 0)
        taps(pc, g, 4, 1)
        run(hooks.get(4, []))

    n = nx * ny
    core = lax.axis_index("dp")
    me = ix * ny + iy
    mesh_id = pl.DeviceIdType.MESH
    pieces, _, _, units, sent = layout(nx, ny, nd, ch)
    kinds = ("pair", "rs", "ag", "fw")
    side = side_of(ny)

    def each(lo, hi, fn):
        if hi - lo <= 3:
            for o in range(lo, hi):
                fn(o)
            return

        def body(o, carry):
            fn(o)
            return carry

        lax.fori_loop(lo, hi, body, 0)

    def group(p):
        return {"sx": p // ny, "sy": lax.rem(p, ny)}

    class Sum:
        def __init__(self, item):
            self.it = item
            self.g = item["g"]
            q = item["q"]
            self.sizes = item["sizes"]
            m = self.m = len(self.sizes)
            if m == 3:
                cx = lax.rem(iy, side)
                cy = lax.div(iy, side)
                first = cx + core * (cy - cx)
                second = cx + cy - first
                self.coords = (first, second, ix)
                self.other = second
                self.steps = (1 + core * (side - 1), side - core * (side - 1))
            elif m == 2:
                self.coords = (iy, ix)
                self.other = iy
                self.steps = (1,)
            else:
                self.coords = (me,)
                self.other = me
            self.size = [n * q]
            self.off = [0]
            for l in range(m):
                self.size.append(self.size[-1] // self.sizes[l])
                self.off.append(self.off[-1] + self.coords[l] * self.size[-1])
            self.hb = item["base"] // nd
            self.mine = item["base"] + core * (n * q)
            self.theirs = item["base"] + (1 - core) * (n * q)
            self.whole = item["whole"]

        def to(self, l, o):
            c = self.coords[l]
            p = lax.rem(c + o, self.sizes[l])
            if self.m == 1:
                return p, group(p)
            if l == self.m - 1:
                return p, {"sx": p}
            return p, {"sy": iy + (p - c) * self.steps[l]}

        def frm(self, l, o):
            return lax.rem(self.coords[l] + self.sizes[l] - o, self.sizes[l])

        def copy(self, src, dst, kind, k, dev):
            return pltpu.make_async_remote_copy(
                src_ref=src,
                dst_ref=dst,
                send_sem=sum_send.at[4 * self.g + kinds.index(kind)],
                recv_sem=sum_recv.at[k],
                device_id=dev,
                device_id_type=mesh_id,
            )

        def pair(self):
            return self.copy(
                gb.at[self.g, pl.ds(self.theirs, self.size[0])],
                dx_buf.at[self.g, pl.ds(self.hb, self.size[0])],
                "pair",
                self.it["pair"],
                {"dp": 1 - core},
            )

        def last(self, l):
            return self.whole and l == self.m - 1

        def rs(self, l, o):
            p, dev = self.to(l, o)
            room, step = self.it["slot"][l]
            at = self.off[l] if self.last(l) else self.off[l] + p * step
            return self.copy(
                hs.at[self.g, pl.ds(self.hb + at, step)],
                rb.at[pl.ds(room + o * step, step)],
                "rs",
                self.it["rs"][l],
                dev,
            )

        def rs_wait(self, l):
            room, step = self.it["slot"][l]
            _, dev = self.to(l, 1)
            here = rb.at[pl.ds(room + step, (self.sizes[l] - 1) * step)]
            self.copy(here, here, "rs", self.it["rs"][l], dev).wait_recv()

        def ag(self, l, o, owner):
            _, dev = self.to(l, o)
            size = self.size[l + 1]
            here = pl.ds(self.mine + self.off[l] + owner * size, size)
            k = self.it["ag"][l] + (o if l == 0 else 0)
            return self.copy(fin.at[self.g, here], fin.at[self.g, here], "ag", k, dev)

        def ag_wait(self, l):
            size = self.size[l + 1]
            _, dev = self.to(l, 1)
            here = fin.at[self.g, pl.ds(self.mine + self.off[l], (self.sizes[l] - 1) * size)]
            self.copy(here, here, "ag", self.it["ag"][l], dev).wait_recv()

        def fw(self, o, base, c):
            size = self.size[1]
            here = pl.ds(base + lax.rem(c + self.sizes[0] - o, self.sizes[0]) * size, size)
            return self.copy(fin.at[self.g, here], fin.at[self.g, here], "fw", self.it["fw"], {"dp": 1 - core})

        def begin(self):
            self.pair().start()

        def total(self, l, at, size):
            own = hs[self.g, pl.ds(self.hb + at, size)] if l >= 0 else gb[self.g, pl.ds(self.mine + at, size)]
            v = own.astype(F32)
            if l < 0:
                return v + dx_buf[self.g, pl.ds(self.hb + at, size)].astype(F32)
            room, step = self.it["slot"][l]
            back = at - self.off[l + 1]

            def add(o, acc):
                return acc + rb[pl.ds(room + o * step + back, size)].astype(F32)

            if self.sizes[l] <= 4:
                for o in range(1, self.sizes[l]):
                    v = add(o, v)
                return v
            return lax.fori_loop(1, self.sizes[l], add, v)

        def reduce(self, l):
            if l < 0:
                self.pair().wait_recv()
            else:
                self.rs_wait(l)
            nxt = l + 1
            if nxt == self.m:
                size = self.size[self.m]
                v = self.total(l, self.off[self.m], size)
                fin[self.g, pl.ds(self.mine + self.off[self.m], size)] = v.astype(BF16)
                self.share(l)
                return
            room, step = self.it["slot"][nxt]
            if self.last(nxt):
                v = self.total(l, self.off[nxt], step).astype(BF16)
                hs[self.g, pl.ds(self.hb + self.off[nxt], step)] = v
                rb[pl.ds(room, step)] = v
                each(1, self.sizes[nxt], lambda o: self.rs(nxt, o).start())
                return

            def one(o):
                at = self.off[nxt] + lax.rem(self.coords[nxt] + o, self.sizes[nxt]) * step
                hs[self.g, pl.ds(self.hb + at, step)] = self.total(l, at, step).astype(BF16)

            def go(o):
                one(o)
                self.rs(nxt, o).start()

            each(1, self.sizes[nxt], go)
            one(0)

        def settle(self):
            l = self.m - 1
            self.rs_wait(l)
            room, step = self.it["slot"][l]

            def part(p):
                return rb[pl.ds(room + self.frm(l, p) * step, step)].astype(F32)

            v = part(0)
            if self.sizes[l] <= 4:
                for p in range(1, self.sizes[l]):
                    v = v + part(p)
            else:
                v = lax.fori_loop(1, self.sizes[l], lambda p, acc: acc + part(p), v)
            fin[self.g, pl.ds(self.mine + self.off[l], step)] = v.astype(BF16)
            self.share(l - 1)

        def share(self, l):
            each(1, self.sizes[l], lambda o: self.ag(l, o, self.coords[l]).start())
            if l == 0:
                self.fw(0, self.mine, self.coords[0]).start()

        def gather(self, l):
            if l > 0:
                self.ag_wait(l)
                self.share(l - 1)
                return

            def one(o):
                self.ag(l, o, self.frm(l, o)).wait_recv()
                self.fw(o, self.mine, self.coords[0]).start()

            each(1, self.sizes[l], one)

        def arrive(self):
            here = fin.at[self.g, pl.ds(self.theirs, self.size[0])]
            self.copy(here, here, "fw", self.it["fw"], {"dp": 1 - core}).wait_recv()

        def stages(self):
            out = [self.begin]
            for l in range(-1, self.m - (1 if self.whole else 0)):
                out.append(functools.partial(self.reduce, l))
            if self.whole:
                out.append(self.settle)
            for l in reversed(range(self.m - (1 if self.whole else 0))):
                out.append(functools.partial(self.gather, l))
            out.append(self.arrive)
            return out

    sums = [Sum(item) for item in pieces]
    queue = {(s.g, s.it["b"]): s.stages() for s in sums}

    points = {}
    for s in sums:
        k = (s.g, s.it["b"])
        names = STEPS[k]
        for at, fn in enumerate(queue[k]):
            points.setdefault(names[at] if at < len(names) else "end", []).append((at, fn))

    def at(name):
        return [fn for _, fn in points.get(name, [])]

    def hooks_of(name, count):
        return {i: at(name + "." + str(i)) for i in range(count) if at(name + "." + str(i))}

    def run(fns):
        for fn in fns:
            fn()

    def finish(g, ref):
        per = ch // UNIT
        for k in range(27):
            a, b, c = k // 9, k // 3 % 3, k % 3
            j = (b * 3 + c) * 3 + a
            pltpu.make_async_copy(
                fin.at[g, j * per : (j + 1) * per], ref.at[k * per : (k + 1) * per], save_sem.at[2 + g]
            ).start()

    def finished(g, ref):
        count = 27 * (ch // UNIT)
        pltpu.make_async_copy(fin.at[g, 0:count], ref.at[0:count], save_sem.at[2 + g]).wait()

    barrier = pltpu.get_barrier_semaphore()
    each(
        1,
        n,
        lambda o: pl.semaphore_signal(
            barrier, inc=1, device_id=group(lax.rem(me + o, n)), device_id_type=mesh_id
        ),
    )
    pl.semaphore_signal(barrier, inc=1, device_id={"dp": 1 - core}, device_id_type=mesh_id)

    loads = [
        pltpu.make_async_copy(a, b, load_sem.at[s])
        for s, (a, b) in enumerate(((feat_in, feat), (w2_in, w2), (w1_in, w1), (cot_in, cot)))
    ]
    for load in loads:
        load.start()

    for dx, dy in DIRS:
        @pl.when(jnp.logical_not(there(dx, dy)))
        def _(dx=dx, dy=dy):
            for f in range(4):
                r = halo_ref(f, dx, dy)
                r[...] = jnp.zeros(r.shape, BF16)

    spare = units - 27 * (ch // UNIT)
    if spare:
        for g in range(2):
            gb[g, units - spare :] = jnp.zeros((spare, UNIT, ch), BF16)

    slots = rows // edge
    row = lax.broadcasted_iota(jnp.int32, (plane, ch), 0)
    live[...] = jnp.where(lax.rem(lax.div(row, edge), slots) < count[0], 1.0, 0.0).astype(F32)

    r = lax.broadcasted_iota(jnp.int32, (3 * rows, rows), 0)
    col = lax.broadcasted_iota(jnp.int32, (3 * rows, rows), 1)
    src = lax.rem(r, edge) + lax.div(r, rows) - 1
    dz = jnp.where(src < 0, 0, jnp.where(src >= edge, 2, 1))
    key = dz * slots + lax.rem(lax.div(r, edge), slots)
    same_z = lax.rem(src + edge, edge) == lax.rem(col, edge)
    slot = lax.div(col, edge)
    for d in range(9):
        target = jnp.full((3 * rows, rows), -1, jnp.int32)
        for k in range(3):
            way = d * 3 + k
            for sl in range(slots):
                name = sl if way == 13 else nb[sl, way if way < 13 else way - 1]
                target = jnp.where(key == k * slots + sl, name, target)
        hit = jnp.logical_and(same_z, target == slot)
        sel[d] = jnp.where(hit, 1.0, 0.0).astype(F32).astype(BF16)

    def flip(w, to):
        def body(k, carry):
            to[k] = w[26 - k].astype(F32).T.astype(BF16)
            return carry

        lax.fori_loop(0, 27, body, 0)

    def mask_in(x, carry):
        v = feat[x].astype(F32).reshape(plane, ch) * live[...]
        fld[0, x] = v.astype(BF16).reshape(edge, rows, ch)
        return carry

    loads[0].wait()
    lax.fori_loop(0, edge, mask_in, 0)

    pl.semaphore_wait(barrier, n)

    def store(f, x, v):
        fld[f, x] = v.astype(BF16).reshape(edge, rows, ch)

    send(0)
    inner(0, pc_a)
    loads[1].wait()
    flip(w2, w2f)
    loads[2].wait()
    arrive(0)
    outer(0, pc_a)

    def use1(i, h, v):
        x = 2 * i + h
        pre[x] = v
        store(1, x, v * jax.nn.sigmoid(v) * live[...])

    def halo_1(i, dx):
        def go():
            if dx:
                send(1, lambda x, y: x == dx)
            send(1, side_y, (2 * i, 2 * i + 2))

        return [go]

    last = pairs - 1
    hooks = {(i + 1) % pairs: halo_1(i, {0: -1, last: 1}.get(i, 0)) for i in range(pairs)}
    conv(pc_a, w1, use1, hooks, last)
    inner(1, pc_b)
    flip(w1, w1f)
    arrive(1, lambda x, y: x != 0)
    arrive_y(1, False, 0, edge - 2)
    outer_x(1, pc_b)
    outer_y(1, pc_b, [x for x in range(edge) if x not in (late, late + 1)])
    loads[3].wait()

    def rest_1():
        arrive_y(1, True, late, late + 2)
        outer_y(1, pc_b, [late, late + 1])

    def use2(i, h, v):
        x = 2 * i + h
        v = v + fld[0, x].reshape(plane, ch).astype(F32)
        s = jax.nn.sigmoid(v)
        out_ref[x] = (v * s * live[...]).astype(BF16).reshape(edge, rows, ch)
        g = cot[x].reshape(plane, ch).astype(F32) * (s * (1.0 + v * (1.0 - s))) * live[...]
        store(2, x, g)
        keep_t(i, h, g)

    conv(pc_b, w2, use2, {0: [rest_1]})
    save_out = pltpu.make_async_copy(out_ref, out_hbm, save_sem.at[0])
    save_out.start()
    send(2)
    inner(2, pc_c)
    wgrad(pc_b, 0, hooks_of("w2", 5))
    arrive(2)
    outer(2, pc_c)
    run(at("o2"))

    def use3(i, h, v):
        x = 2 * i + h
        g = v * slope(pre[x]) * live[...]
        store(3, x, g)
        keep_t(i, h, g)

    conv(pc_c, w2f, use3, hooks_of("c3", pairs))
    send(3)
    wgrad(pc_a, 1, hooks_of("w1", 5))
    inner(3, pc_c)
    arrive(3)
    outer(3, pc_c)
    run(at("o3"))

    def use4(i, h, v):
        x = 2 * i + h
        g = (fld[2, x].reshape(plane, ch).astype(F32) + v) * live[...]
        gin_ref[x] = g.astype(BF16).reshape(edge, rows, ch)

    conv(pc_c, w1f, use4, hooks_of("c4", pairs))
    save_gin = pltpu.make_async_copy(gin_ref, gin_hbm, save_sem.at[1])
    save_gin.start()
    for _, fn in sorted(points.get("end", []), key=lambda e: e[0]):
        fn()
    finish(0, gw2_hbm)
    finish(1, gw1_hbm)
    save_out.wait()
    save_gin.wait()
    finished(0, gw2_hbm)
    finished(1, gw1_hbm)
    for f in range(4):
        drain(f)
    for (g, kind), count in sent.items():
        here = gb.at[g, pl.ds(0, count)]
        pltpu.make_async_remote_copy(
            src_ref=here,
            dst_ref=here,
            send_sem=sum_send.at[4 * g + kinds.index(kind)],
            recv_sem=sum_recv.at[0],
            device_id={"dp": 1 - core},
            device_id_type=mesh_id,
        ).wait_send()


def shards(nx, ny, nd, features, cotangent, first_weight, second_weight, neighbours, counts):
    _, edge, _, slots, _, ch = features.shape
    rows = slots * edge
    plane = edge * rows
    flat = (edge, edge, rows, ch)
    scale = float(nx * ny * nd * slots * edge**3) ** -0.5
    hbm = pl.BlockSpec(memory_space=pl.ANY)
    smem = pl.BlockSpec(memory_space=pltpu.SMEM)
    _, nsem, room, units, _ = layout(nx, ny, nd, ch)
    gshape = jax.ShapeDtypeStruct((units, UNIT, ch), BF16)
    fshape = jax.ShapeDtypeStruct(flat, BF16)
    out, gin, g1, g2 = pl.pallas_call(
        functools.partial(kernel, nx, ny, nd),
        out_shape=[fshape, fshape, gshape, gshape],
        in_specs=[hbm] * 4 + [smem] * 2,
        out_specs=[hbm] * 4,
        scratch_shapes=[
            pltpu.VMEM(flat, BF16),
            pltpu.VMEM(flat, BF16),
            pltpu.VMEM((27, ch, ch), BF16),
            pltpu.VMEM((27, ch, ch), BF16),
            pltpu.VMEM(flat, BF16),
            pltpu.VMEM(flat, BF16),
            pltpu.SemaphoreType.DMA((4,)),
            pltpu.SemaphoreType.DMA((4,)),
            pltpu.VMEM((4,) + flat, BF16),
            pltpu.VMEM((4, 2, edge, rows, ch), BF16),
            pltpu.VMEM((4, 2, edge, rows, ch), BF16),
            pltpu.VMEM((4, 4, rows, ch), BF16),
            pltpu.VMEM((edge + 2, edge, rows, 9 * ch), BF16),
            pltpu.VMEM((edge + 2, edge, rows, 9 * ch), BF16),
            pltpu.VMEM((edge + 2, edge, rows, 9 * ch), BF16),
            pltpu.VMEM((edge, plane, ch), F32),
            pltpu.VMEM((3 * ch, (edge + 2) * plane), BF16),
            pltpu.SemaphoreType.DMA((4, len(DIRS))),
            pltpu.SemaphoreType.DMA((4, len(DIRS) + 2)),
            pltpu.VMEM((27, ch, ch), BF16),
            pltpu.VMEM((27, ch, ch), BF16),
            pltpu.VMEM((9, 3 * rows, rows), BF16),
            pltpu.VMEM((plane, ch), F32),
            pltpu.VMEM((2, units, UNIT, ch), BF16),
            pltpu.VMEM((2, units // nd, UNIT, ch), BF16),
            pltpu.VMEM((2, units // nd, UNIT, ch), BF16),
            pltpu.VMEM((room, UNIT, ch), BF16),
            pltpu.VMEM((2, units, UNIT, ch), BF16),
            pltpu.SemaphoreType.DMA((8,)),
            pltpu.SemaphoreType.DMA((nsem,)),
        ],
        compiler_params=pltpu.CompilerParams(
            collective_id=0, has_side_effects=True, vmem_limit_bytes=60 * 1024 * 1024
        ),
    )(
        features.reshape(flat),
        cotangent.reshape(flat),
        first_weight,
        second_weight,
        neighbours[0, 0, 0],
        counts.reshape(1),
    )
    def finish(g):
        g = g.reshape(-1, ch)[: 27 * ch]
        return g.reshape(27, ch, ch).astype(F32) * scale

    return out.reshape(features.shape), gin.reshape(features.shape), finish(g1), finish(g2)


def solution(mesh):
    field = P("dp", "sx", "sy", None, None, None)
    return jax.shard_map(
        functools.partial(shards, mesh.shape["sx"], mesh.shape["sy"], mesh.shape["dp"]),
        mesh=mesh,
        in_specs=(field, field, P(), P(), P("dp", "sx", "sy", None, None), P("dp", "sx", "sy")),
        out_specs=(field, field, P(), P()),
        check_vma=False,
    )
```

```python
import functools

import jax
import jax.numpy as jnp
from jax import lax
from jax.experimental import pallas as pl
from jax.experimental.pallas import tpu as pltpu
from jax.sharding import PartitionSpec as P

DIRS = [(dx, dy) for dx in (-1, 0, 1) for dy in (-1, 0, 1) if (dx, dy) != (0, 0)]
F32 = jnp.float32
BF16 = jnp.bfloat16
UNIT = 16


def slope(v):
    s = jax.nn.sigmoid(v)
    return s * (1.0 + v * (1.0 - s))


MODES = (
    ("yz", "yz", "yz", "yz", "yz"),
    ("yz", "yz", "yz", "yzw", "yzw"),
)
STEPS = {
    (0, 0): ("w2.0", "w2.2", "c3.3", "w1.4", "c4.2"),
    (0, 1): ("w2.1", "w2.3", "c3.3", "w1.4", "c4.2"),
    (0, 2): ("w2.2", "w2.4", "c3.3", "w1.4", "c4.2"),
    (0, 3): ("w2.3", "o2", "w1.0", "o3", "c4.2"),
    (0, 4): ("w2.4", "c3.0", "w1.1", "o3", "c4.2"),
    (1, 0): ("w1.0", "w1.2", "c4.1"),
    (1, 1): ("w1.1", "w1.3", "c4.1"),
    (1, 2): ("w1.2", "w1.4", "c4.1"),
    (1, 3): ("w1.3", "o3", "c4.3"),
    (1, 4): ("w1.4", "o3", "c4.3"),
}


def side_of(ny):
    f = 1
    while f * f < ny:
        f += 1
    return f if f * f == ny else None


def layout(nx, ny, nd, ch):
    n = nx * ny
    total = -(-27 * ch // (UNIT * n * nd))
    pieces = []
    sems = 0
    room = 0
    out = {}

    def sent(g, kind, count):
        out[g, kind] = out.get((g, kind), 0) + count

    for g in range(2):
        f = side_of(ny)
        done = 0
        for b in range(5):
            upto = total if b == 4 else min((b + 1) * (6 * ch // UNIT) // (n * nd), total)
            q = upto - done
            if q <= 0:
                continue
            mode = MODES[g][b]
            whole = mode[-1] == "w"
            if mode == "all":
                sizes = (n,)
            elif mode[:3] == "abz" and f:
                sizes = (f, f, nx)
            else:
                sizes = (ny, nx)
            item = dict(g=g, b=b, q=q, base=done * n * nd, sizes=sizes, whole=whole, rs=[], ag=[], slot=[])
            item["pair"] = sems
            sems += 1
            left = n * q
            sent(g, "pair", left)
            for l, s in enumerate(sizes):
                last = whole and l == len(sizes) - 1
                step = left if last else left // s
                item["rs"].append(sems)
                sems += 1
                sent(g, "rs", (s - 1) * step)
                item["ag"].append(sems)
                if l == 0:
                    sems += s
                elif not last:
                    sems += 1
                if not last:
                    sent(g, "ag", (s - 1) * step)
                item["slot"].append((room, step))
                room += s * step
                left = left // s
            item["fw"] = sems
            sems += 1
            sent(g, "fw", n * q)
            pieces.append(item)
            done = upto
    return pieces, sems, room, total * n * nd, out


def kernel(
    nx,
    ny,
    nd,
    feat_in,
    cot_in,
    w1_in,
    w2_in,
    nb,
    count,
    out_hbm,
    gin_hbm,
    gw1_hbm,
    gw2_hbm,
    feat,
    cot,
    w1,
    w2,
    out_ref,
    gin_ref,
    load_sem,
    save_sem,
    fld,
    rx,
    ry,
    rc,
    pc_a,
    pc_b,
    pc_c,
    pre,
    gt,
    send_sem,
    recv_sem,
    w1f,
    w2f,
    sel,
    live,
    gb,
    dx_buf,
    hs,
    rb,
    fin,
    sum_send,
    sum_recv,
):
    edge = feat.shape[0]
    rows = feat.shape[2]
    ch = feat.shape[3]
    pairs = edge // 2
    plane = edge * rows
    ix = lax.axis_index("sx")
    iy = lax.axis_index("sy")

    def there(dx, dy):
        ok = None
        for d, i, n in ((dx, ix, nx), (dy, iy, ny)):
            if d == 0:
                continue
            c = (i < n - 1) if d > 0 else (i > 0)
            ok = c if ok is None else jnp.logical_and(ok, c)
        return ok

    def peer(dx, dy):
        px = jnp.minimum(jnp.maximum(ix + dx, 0), nx - 1)
        py = jnp.minimum(jnp.maximum(iy + dy, 0), ny - 1)
        return {"sx": px, "sy": py}

    def halo_ref(f, dx, dy):
        if dy == 0:
            return rx.at[f, (dx + 1) // 2]
        if dx == 0:
            return ry.at[f, (dy + 1) // 2]
        return rc.at[f, (dx + 1) // 2 * 2 + (dy + 1) // 2]

    late = 2 * (pairs - 2)

    def desc(f, k, part=None):
        dx, dy = DIRS[k]
        far_x = edge - 1 if dx > 0 else 0
        far_y = edge - 1 if dy > 0 else 0
        dst = halo_ref(f, -dx, -dy)
        wait = k
        if dy == 0:
            src = fld.at[f, far_x]
        elif dx == 0:
            src = fld.at[f, :, far_y]
            if part is not None:
                lo, hi = part
                src = fld.at[f, lo:hi, far_y]
                dst = dst.at[lo:hi]
                if lo == late:
                    wait = len(DIRS) + (dy + 1) // 2
        else:
            src = fld.at[f, far_x, far_y]
        return pltpu.make_async_remote_copy(
            src_ref=src,
            dst_ref=dst,
            send_sem=send_sem.at[f, k],
            recv_sem=recv_sem.at[f, wait],
            device_id=peer(dx, dy),
            device_id_type=pl.DeviceIdType.MESH,
        )

    def send(f, keep=lambda dx, dy: True, part=None):
        for k, (dx, dy) in enumerate(DIRS):
            if keep(dx, dy):
                @pl.when(there(dx, dy))
                def _(k=k):
                    desc(f, k, part).start()

    def arrive(f, keep=lambda dx, dy: True):
        for k, (dx, dy) in enumerate(DIRS):
            if keep(dx, dy):
                @pl.when(there(-dx, -dy))
                def _(k=k):
                    desc(f, k).wait_recv()

    def side_y(dx, dy):
        return dx == 0

    def arrive_y(f, part, lo, hi):
        for k, (dx, dy) in enumerate(DIRS):
            if dx == 0:
                @pl.when(there(-dx, -dy))
                def _(k=k, dy=dy):
                    here = halo_ref(f, 0, -dy).at[lo:hi]
                    pltpu.make_async_remote_copy(
                        src_ref=here,
                        dst_ref=here,
                        send_sem=send_sem.at[f, k],
                        recv_sem=recv_sem.at[f, len(DIRS) + (dy + 1) // 2 if part else k],
                        device_id=peer(0, dy),
                        device_id_type=pl.DeviceIdType.MESH,
                    ).wait_recv()

    def drain(f):
        for k, (dx, dy) in enumerate(DIRS):
            @pl.when(there(dx, dy))
            def _(k=k):
                desc(f, k).wait_send()

    def put(pc, x, yp, tile):
        t = tile.astype(BF16)
        for b in range(3):
            y = yp - b
            if 0 <= y < edge:
                for c in range(3):
                    lo = (b * 3 + c) * ch
                    pc[x, y, :, lo : lo + ch] = t[c * rows : (c + 1) * rows]

    def line(pc, x, s, tiles):
        cat = jnp.concatenate(tiles, axis=1)
        got = jnp.dot(s, cat, preferred_element_type=F32)
        for y in range(edge):
            put(pc, x, y + 1, got[:, y * ch : (y + 1) * ch])

    def inner(f, pc):
        def body(x, carry):
            line(pc, x + 1, sel[4], [fld[f, x, y] for y in range(edge)])
            return carry

        lax.fori_loop(0, edge, body, 0)

    def outer_x(f, pc):
        for h in range(2):
            x = 0 if h == 0 else edge + 1
            line(pc, x, sel[6 * h + 1], [rx[f, h, y] for y in range(edge)])
            for g in range(2):
                yp = 0 if g == 0 else edge + 1
                put(pc, x, yp, jnp.dot(sel[6 * h + 2 * g], rc[f, h * 2 + g], preferred_element_type=F32))

    def outer_y(f, pc, xs):
        for h in range(2):
            cat = jnp.concatenate([ry[f, h, x] for x in xs], axis=1)
            got = jnp.dot(sel[3 + 2 * h], cat, preferred_element_type=F32)
            for n_x, x in enumerate(xs):
                put(pc, x + 1, 0 if h == 0 else edge + 1, got[:, n_x * ch : (n_x + 1) * ch])

    def outer(f, pc):
        outer_x(f, pc)
        outer_y(f, pc, range(edge))

    def conv(pc, w, use, hooks=None, turn=0):
        def body(step, carry):
            i = lax.rem(step + turn, pairs) if turn else step

            def lhs(p):
                return pc[2 * i + p].reshape(plane, 9 * ch)

            def tap(a):
                return w[9 * a : 9 * a + 9].reshape(9 * ch, ch)

            low = jnp.concatenate([tap(1), tap(0)], axis=1)
            high = jnp.concatenate([tap(2), tap(1)], axis=1)
            both = jnp.dot(
                jnp.concatenate([lhs(1), lhs(2)], axis=1),
                jnp.concatenate([low, high], axis=0),
                preferred_element_type=F32,
            )
            left = both[:, :ch] + jnp.dot(lhs(0), tap(0), preferred_element_type=F32)
            right = both[:, ch:] + jnp.dot(lhs(3), tap(2), preferred_element_type=F32)
            use(i, 0, left)
            use(i, 1, right)
            hooked(step, hooks)
            return carry

        lax.fori_loop(0, pairs, body, 0)

    def keep_t(i, h, v):
        t = v.T.astype(BF16)
        for a in range(3):
            at = pl.multiple_of((2 * i + h + a) * plane, plane)
            gt[a * ch : (a + 1) * ch, pl.ds(at, plane)] = t

    def tap_out(g, j, wide, v):
        per = ch // UNIT
        for s in range(wide):
            for a in range(3):
                t = v[a][:, s * ch : (s + 1) * ch].T.astype(BF16).reshape(per, UNIT, ch)
                gb[g, pl.ds(((2 * j + s) * 3 + a) * per, per)] = t

    def hooked(i, hooks):
        for at, fns in sorted((hooks or {}).items()):
            @pl.when(i == at)
            def _(fns=fns):
                for fn in fns:
                    fn()

    def taps(pc, g, j, wide):
        lanes = pl.ds(pl.multiple_of(j * (2 * ch), 2 * ch), wide * ch)

        def part(lo, hi, x0, x1):
            rhs = pc[x0:x1, :, :, lanes].reshape((x1 - x0) * plane, wide * ch)
            lhs = gt[lo * ch : hi * ch, x0 * plane : x1 * plane]
            return jnp.dot(lhs, rhs, preferred_element_type=F32)

        mid = part(0, 3, 2, edge)
        low = part(0, 2, 1, 2)
        high = part(1, 3, edge, edge + 1)
        rows3 = (
            mid[:ch] + low[:ch] + part(0, 1, 0, 1),
            mid[ch : 2 * ch] + low[ch:] + high[:ch],
            mid[2 * ch :] + high[ch:] + part(2, 3, edge + 1, edge + 2),
        )
        tap_out(g, j, wide, rows3)

    def wgrad(pc, g, hooks):
        def body(j, carry):
            taps(pc, g, j, 2)
            hooked(j, hooks)
            return carry

        lax.fori_loop(0, 4, body, 0)
        taps(pc, g, 4, 1)
        run(hooks.get(4, []))

    n = nx * ny
    core = lax.axis_index("dp")
    me = ix * ny + iy
    mesh_id = pl.DeviceIdType.MESH
    pieces, _, _, units, sent = layout(nx, ny, nd, ch)
    kinds = ("pair", "rs", "ag", "fw")
    side = side_of(ny)

    def each(lo, hi, fn):
        if hi - lo <= 3:
            for o in range(lo, hi):
                fn(o)
            return

        def body(o, carry):
            fn(o)
            return carry

        lax.fori_loop(lo, hi, body, 0)

    def group(p):
        return {"sx": p // ny, "sy": lax.rem(p, ny)}

    class Sum:
        def __init__(self, item):
            self.it = item
            self.g = item["g"]
            q = item["q"]
            self.sizes = item["sizes"]
            m = self.m = len(self.sizes)
            if m == 3:
                cx = lax.rem(iy, side)
                cy = lax.div(iy, side)
                first = cx + core * (cy - cx)
                second = cx + cy - first
                self.coords = (first, second, ix)
                self.other = second
                self.steps = (1 + core * (side - 1), side - core * (side - 1))
            elif m == 2:
                self.coords = (iy, ix)
                self.other = iy
                self.steps = (1,)
            else:
                self.coords = (me,)
                self.other = me
            self.size = [n * q]
            self.off = [0]
            for l in range(m):
                self.size.append(self.size[-1] // self.sizes[l])
                self.off.append(self.off[-1] + self.coords[l] * self.size[-1])
            self.hb = item["base"] // nd
            self.mine = item["base"] + core * (n * q)
            self.theirs = item["base"] + (1 - core) * (n * q)
            self.whole = item["whole"]

        def to(self, l, o):
            c = self.coords[l]
            p = lax.rem(c + o, self.sizes[l])
            if self.m == 1:
                return p, group(p)
            if l == self.m - 1:
                return p, {"sx": p}
            return p, {"sy": iy + (p - c) * self.steps[l]}

        def frm(self, l, o):
            return lax.rem(self.coords[l] + self.sizes[l] - o, self.sizes[l])

        def copy(self, src, dst, kind, k, dev):
            return pltpu.make_async_remote_copy(
                src_ref=src,
                dst_ref=dst,
                send_sem=sum_send.at[4 * self.g + kinds.index(kind)],
                recv_sem=sum_recv.at[k],
                device_id=dev,
                device_id_type=mesh_id,
            )

        def pair(self):
            return self.copy(
                gb.at[self.g, pl.ds(self.theirs, self.size[0])],
                dx_buf.at[self.g, pl.ds(self.hb, self.size[0])],
                "pair",
                self.it["pair"],
                {"dp": 1 - core},
            )

        def last(self, l):
            return self.whole and l == self.m - 1

        def rs(self, l, o):
            p, dev = self.to(l, o)
            room, step = self.it["slot"][l]
            at = self.off[l] if self.last(l) else self.off[l] + p * step
            return self.copy(
                hs.at[self.g, pl.ds(self.hb + at, step)],
                rb.at[pl.ds(room + o * step, step)],
                "rs",
                self.it["rs"][l],
                dev,
            )

        def rs_wait(self, l):
            room, step = self.it["slot"][l]
            _, dev = self.to(l, 1)
            here = rb.at[pl.ds(room + step, (self.sizes[l] - 1) * step)]
            self.copy(here, here, "rs", self.it["rs"][l], dev).wait_recv()

        def ag(self, l, o, owner):
            _, dev = self.to(l, o)
            size = self.size[l + 1]
            here = pl.ds(self.mine + self.off[l] + owner * size, size)
            k = self.it["ag"][l] + (o if l == 0 else 0)
            return self.copy(fin.at[self.g, here], fin.at[self.g, here], "ag", k, dev)

        def ag_wait(self, l):
            size = self.size[l + 1]
            _, dev = self.to(l, 1)
            here = fin.at[self.g, pl.ds(self.mine + self.off[l], (self.sizes[l] - 1) * size)]
            self.copy(here, here, "ag", self.it["ag"][l], dev).wait_recv()

        def fw(self, o, base, c):
            size = self.size[1]
            here = pl.ds(base + lax.rem(c + self.sizes[0] - o, self.sizes[0]) * size, size)
            return self.copy(fin.at[self.g, here], fin.at[self.g, here], "fw", self.it["fw"], {"dp": 1 - core})

        def begin(self):
            self.pair().start()

        def total(self, l, at, size):
            own = hs[self.g, pl.ds(self.hb + at, size)] if l >= 0 else gb[self.g, pl.ds(self.mine + at, size)]
            v = own.astype(F32)
            if l < 0:
                return v + dx_buf[self.g, pl.ds(self.hb + at, size)].astype(F32)
            room, step = self.it["slot"][l]
            back = at - self.off[l + 1]

            def add(o, acc):
                return acc + rb[pl.ds(room + o * step + back, size)].astype(F32)

            if self.sizes[l] <= 4:
                for o in range(1, self.sizes[l]):
                    v = add(o, v)
                return v
            return lax.fori_loop(1, self.sizes[l], add, v)

        def reduce(self, l):
            if l < 0:
                self.pair().wait_recv()
            else:
                self.rs_wait(l)
            nxt = l + 1
            if nxt == self.m:
                size = self.size[self.m]
                v = self.total(l, self.off[self.m], size)
                fin[self.g, pl.ds(self.mine + self.off[self.m], size)] = v.astype(BF16)
                self.share(l)
                return
            room, step = self.it["slot"][nxt]
            if self.last(nxt):
                v = self.total(l, self.off[nxt], step).astype(BF16)
                hs[self.g, pl.ds(self.hb + self.off[nxt], step)] = v
                rb[pl.ds(room, step)] = v
                each(1, self.sizes[nxt], lambda o: self.rs(nxt, o).start())
                return

            def one(o):
                at = self.off[nxt] + lax.rem(self.coords[nxt] + o, self.sizes[nxt]) * step
                hs[self.g, pl.ds(self.hb + at, step)] = self.total(l, at, step).astype(BF16)

            def go(o):
                one(o)
                self.rs(nxt, o).start()

            each(1, self.sizes[nxt], go)
            one(0)

        def settle(self):
            l = self.m - 1
            self.rs_wait(l)
            room, step = self.it["slot"][l]

            def part(p):
                return rb[pl.ds(room + self.frm(l, p) * step, step)].astype(F32)

            v = part(0)
            if self.sizes[l] <= 4:
                for p in range(1, self.sizes[l]):
                    v = v + part(p)
            else:
                v = lax.fori_loop(1, self.sizes[l], lambda p, acc: acc + part(p), v)
            fin[self.g, pl.ds(self.mine + self.off[l], step)] = v.astype(BF16)
            self.share(l - 1)

        def share(self, l):
            each(1, self.sizes[l], lambda o: self.ag(l, o, self.coords[l]).start())
            if l == 0:
                self.fw(0, self.mine, self.coords[0]).start()

        def gather(self, l):
            if l > 0:
                self.ag_wait(l)
                self.share(l - 1)
                return

            def one(o):
                self.ag(l, o, self.frm(l, o)).wait_recv()
                self.fw(o, self.mine, self.coords[0]).start()

            each(1, self.sizes[l], one)

        def arrive(self):
            here = fin.at[self.g, pl.ds(self.theirs, self.size[0])]
            self.copy(here, here, "fw", self.it["fw"], {"dp": 1 - core}).wait_recv()

        def stages(self):
            out = [self.begin]
            for l in range(-1, self.m - (1 if self.whole else 0)):
                out.append(functools.partial(self.reduce, l))
            if self.whole:
                out.append(self.settle)
            for l in reversed(range(self.m - (1 if self.whole else 0))):
                out.append(functools.partial(self.gather, l))
            out.append(self.arrive)
            return out

    sums = [Sum(item) for item in pieces]
    queue = {(s.g, s.it["b"]): s.stages() for s in sums}

    points = {}
    for s in sums:
        k = (s.g, s.it["b"])
        names = STEPS[k]
        for at, fn in enumerate(queue[k]):
            points.setdefault(names[at] if at < len(names) else "end", []).append((at, fn))

    def at(name):
        return [fn for _, fn in points.get(name, [])]

    def hooks_of(name, count):
        return {i: at(name + "." + str(i)) for i in range(count) if at(name + "." + str(i))}

    def run(fns):
        for fn in fns:
            fn()

    def finish(g, ref):
        per = ch // UNIT
        for k in range(27):
            a, b, c = k // 9, k // 3 % 3, k % 3
            j = (b * 3 + c) * 3 + a
            pltpu.make_async_copy(
                fin.at[g, j * per : (j + 1) * per], ref.at[k * per : (k + 1) * per], save_sem.at[2 + g]
            ).start()

    def finished(g, ref):
        count = 27 * (ch // UNIT)
        pltpu.make_async_copy(fin.at[g, 0:count], ref.at[0:count], save_sem.at[2 + g]).wait()

    barrier = pltpu.get_barrier_semaphore()
    each(
        1,
        n,
        lambda o: pl.semaphore_signal(
            barrier, inc=1, device_id=group(lax.rem(me + o, n)), device_id_type=mesh_id
        ),
    )
    pl.semaphore_signal(barrier, inc=1, device_id={"dp": 1 - core}, device_id_type=mesh_id)

    loads = [
        pltpu.make_async_copy(a, b, load_sem.at[s])
        for s, (a, b) in enumerate(((feat_in, feat), (w2_in, w2), (w1_in, w1), (cot_in, cot)))
    ]
    for load in loads:
        load.start()

    for dx, dy in DIRS:
        @pl.when(jnp.logical_not(there(dx, dy)))
        def _(dx=dx, dy=dy):
            for f in range(4):
                r = halo_ref(f, dx, dy)
                r[...] = jnp.zeros(r.shape, BF16)

    spare = units - 27 * (ch // UNIT)
    if spare:
        for g in range(2):
            gb[g, units - spare :] = jnp.zeros((spare, UNIT, ch), BF16)

    slots = rows // edge
    row = lax.broadcasted_iota(jnp.int32, (plane, ch), 0)
    live[...] = jnp.where(lax.rem(lax.div(row, edge), slots) < count[0], 1.0, 0.0).astype(F32)

    r = lax.broadcasted_iota(jnp.int32, (3 * rows, rows), 0)
    col = lax.broadcasted_iota(jnp.int32, (3 * rows, rows), 1)
    src = lax.rem(r, edge) + lax.div(r, rows) - 1
    dz = jnp.where(src < 0, 0, jnp.where(src >= edge, 2, 1))
    key = dz * slots + lax.rem(lax.div(r, edge), slots)
    same_z = lax.rem(src + edge, edge) == lax.rem(col, edge)
    slot = lax.div(col, edge)
    for d in range(9):
        target = jnp.full((3 * rows, rows), -1, jnp.int32)
        for k in range(3):
            way = d * 3 + k
            for sl in range(slots):
                name = sl if way == 13 else nb[sl, way if way < 13 else way - 1]
                target = jnp.where(key == k * slots + sl, name, target)
        hit = jnp.logical_and(same_z, target == slot)
        sel[d] = jnp.where(hit, 1.0, 0.0).astype(F32).astype(BF16)

    def flip(w, to):
        def body(k, carry):
            to[k] = w[26 - k].astype(F32).T.astype(BF16)
            return carry

        lax.fori_loop(0, 27, body, 0)

    def mask_in(x, carry):
        v = feat[x].astype(F32).reshape(plane, ch) * live[...]
        fld[0, x] = v.astype(BF16).reshape(edge, rows, ch)
        return carry

    loads[0].wait()
    lax.fori_loop(0, edge, mask_in, 0)

    pl.semaphore_wait(barrier, n)

    def store(f, x, v):
        fld[f, x] = v.astype(BF16).reshape(edge, rows, ch)

    send(0)
    inner(0, pc_a)
    loads[1].wait()
    flip(w2, w2f)
    loads[2].wait()
    arrive(0)
    outer(0, pc_a)

    def use1(i, h, v):
        x = 2 * i + h
        pre[x] = v
        store(1, x, v * jax.nn.sigmoid(v) * live[...])

    def halo_1(i, dx):
        def go():
            if dx:
                send(1, lambda x, y: x == dx)
            send(1, side_y, (2 * i, 2 * i + 2))

        return [go]

    last = pairs - 1
    hooks = {(i + 1) % pairs: halo_1(i, {0: -1, last: 1}.get(i, 0)) for i in range(pairs)}
    conv(pc_a, w1, use1, hooks, last)
    inner(1, pc_b)
    flip(w1, w1f)
    arrive(1, lambda x, y: x != 0)
    arrive_y(1, False, 0, edge - 2)
    outer_x(1, pc_b)
    outer_y(1, pc_b, [x for x in range(edge) if x not in (late, late + 1)])
    loads[3].wait()

    def rest_1():
        arrive_y(1, True, late, late + 2)
        outer_y(1, pc_b, [late, late + 1])

    def use2(i, h, v):
        x = 2 * i + h
        v = v + fld[0, x].reshape(plane, ch).astype(F32)
        s = jax.nn.sigmoid(v)
        out_ref[x] = (v * s * live[...]).astype(BF16).reshape(edge, rows, ch)
        g = cot[x].reshape(plane, ch).astype(F32) * (s * (1.0 + v * (1.0 - s))) * live[...]
        store(2, x, g)
        keep_t(i, h, g)

    conv(pc_b, w2, use2, {0: [rest_1]})
    save_out = pltpu.make_async_copy(out_ref, out_hbm, save_sem.at[0])
    save_out.start()
    send(2)
    inner(2, pc_c)
    wgrad(pc_b, 0, hooks_of("w2", 5))
    arrive(2)
    outer(2, pc_c)
    run(at("o2"))

    def use3(i, h, v):
        x = 2 * i + h
        g = v * slope(pre[x]) * live[...]
        store(3, x, g)
        keep_t(i, h, g)

    conv(pc_c, w2f, use3, hooks_of("c3", pairs))
    send(3)
    wgrad(pc_a, 1, hooks_of("w1", 5))
    inner(3, pc_c)
    arrive(3)
    outer(3, pc_c)
    run(at("o3"))

    def use4(i, h, v):
        x = 2 * i + h
        g = (fld[2, x].reshape(plane, ch).astype(F32) + v) * live[...]
        gin_ref[x] = g.astype(BF16).reshape(edge, rows, ch)

    conv(pc_c, w1f, use4, hooks_of("c4", pairs))
    save_gin = pltpu.make_async_copy(gin_ref, gin_hbm, save_sem.at[1])
    save_gin.start()
    for _, fn in sorted(points.get("end", []), key=lambda e: e[0]):
        fn()
    finish(0, gw2_hbm)
    finish(1, gw1_hbm)
    save_out.wait()
    save_gin.wait()
    finished(0, gw2_hbm)
    finished(1, gw1_hbm)
    for f in range(4):
        drain(f)
    for (g, kind), count in sent.items():
        here = gb.at[g, pl.ds(0, count)]
        pltpu.make_async_remote_copy(
            src_ref=here,
            dst_ref=here,
            send_sem=sum_send.at[4 * g + kinds.index(kind)],
            recv_sem=sum_recv.at[0],
            device_id={"dp": 1 - core},
            device_id_type=mesh_id,
        ).wait_send()


def shards(nx, ny, nd, features, cotangent, first_weight, second_weight, neighbours, counts):
    _, edge, _, slots, _, ch = features.shape
    rows = slots * edge
    plane = edge * rows
    flat = (edge, edge, rows, ch)
    scale = float(nx * ny * nd * slots * edge**3) ** -0.5
    hbm = pl.BlockSpec(memory_space=pl.ANY)
    smem = pl.BlockSpec(memory_space=pltpu.SMEM)
    _, nsem, room, units, _ = layout(nx, ny, nd, ch)
    gshape = jax.ShapeDtypeStruct((units, UNIT, ch), BF16)
    fshape = jax.ShapeDtypeStruct(flat, BF16)
    out, gin, g1, g2 = pl.pallas_call(
        functools.partial(kernel, nx, ny, nd),
        out_shape=[fshape, fshape, gshape, gshape],
        in_specs=[hbm] * 4 + [smem] * 2,
        out_specs=[hbm] * 4,
        scratch_shapes=[
            pltpu.VMEM(flat, BF16),
            pltpu.VMEM(flat, BF16),
            pltpu.VMEM((27, ch, ch), BF16),
            pltpu.VMEM((27, ch, ch), BF16),
            pltpu.VMEM(flat, BF16),
            pltpu.VMEM(flat, BF16),
            pltpu.SemaphoreType.DMA((4,)),
            pltpu.SemaphoreType.DMA((4,)),
            pltpu.VMEM((4,) + flat, BF16),
            pltpu.VMEM((4, 2, edge, rows, ch), BF16),
            pltpu.VMEM((4, 2, edge, rows, ch), BF16),
            pltpu.VMEM((4, 4, rows, ch), BF16),
            pltpu.VMEM((edge + 2, edge, rows, 9 * ch), BF16),
            pltpu.VMEM((edge + 2, edge, rows, 9 * ch), BF16),
            pltpu.VMEM((edge + 2, edge, rows, 9 * ch), BF16),
            pltpu.VMEM((edge, plane, ch), F32),
            pltpu.VMEM((3 * ch, (edge + 2) * plane), BF16),
            pltpu.SemaphoreType.DMA((4, len(DIRS))),
            pltpu.SemaphoreType.DMA((4, len(DIRS) + 2)),
            pltpu.VMEM((27, ch, ch), BF16),
            pltpu.VMEM((27, ch, ch), BF16),
            pltpu.VMEM((9, 3 * rows, rows), BF16),
            pltpu.VMEM((plane, ch), F32),
            pltpu.VMEM((2, units, UNIT, ch), BF16),
            pltpu.VMEM((2, units // nd, UNIT, ch), BF16),
            pltpu.VMEM((2, units // nd, UNIT, ch), BF16),
            pltpu.VMEM((room, UNIT, ch), BF16),
            pltpu.VMEM((2, units, UNIT, ch), BF16),
            pltpu.SemaphoreType.DMA((8,)),
            pltpu.SemaphoreType.DMA((nsem,)),
        ],
        compiler_params=pltpu.CompilerParams(
            collective_id=0, has_side_effects=True, vmem_limit_bytes=60 * 1024 * 1024
        ),
    )(
        features.reshape(flat),
        cotangent.reshape(flat),
        first_weight,
        second_weight,
        neighbours[0, 0, 0],
        counts.reshape(1),
    )
    def finish(g):
        g = g.reshape(-1, ch)[: 27 * ch]
        return g.reshape(27, ch, ch).astype(F32) * scale

    return out.reshape(features.shape), gin.reshape(features.shape), finish(g1), finish(g2)


def solution(mesh):
    field = P("dp", "sx", "sy", None, None, None)
    return jax.shard_map(
        functools.partial(shards, mesh.shape["sx"], mesh.shape["sy"], mesh.shape["dp"]),
        mesh=mesh,
        in_specs=(field, field, P(), P(), P("dp", "sx", "sy", None, None), P("dp", "sx", "sy")),
        out_specs=(field, field, P(), P()),
        check_vma=False,
    )
```
